32 devices in a mesh: gx: 4 (over y, x), gz: 4 (over z), gy: 2 (over core).
Axes of the slice: x: 2, y: 2, z: 4, core: 2. Of those that a mesh axis runs over, the one named last changes fastest.
Arguments:
- blocks: bfloat16 [4, 4, 4, 96, 4096], P('gx', 'gz', 'gy'), may hold values from -6 to 6
- block_count: int32 [4, 4, 2], P('gx', 'gz', 'gy'), may hold values from 1 to 2, as said below
- neighbours: int32 [4, 4, 4, 26], P('gx', 'gz', 'gy'), may hold values from -1 to 15, as said below
- conv_weight: bfloat16 [48, 2592], replicated, may hold values from -0.125 to 0.125
- conv_bias: float32 [48], replicated, may hold values from -3 to 3
- head_weight: bfloat16 [48, 48], replicated, may hold values from -0.875 to 0.875
- head_bias: float32 [48], replicated, may hold values from -3 to 3
Outputs:
- features: bfloat16 [4, 4, 4, 48, 4096], P('gx', 'gz', 'gy')
The draws below stay inside these ranges and needn't reach their ends.
Inputs may be any that keep to these rules, and one draw needn't show every extreme that they name: Each device's foreground blocks fill its first block_count slots; some device fills all 2. `neighbours`: -1 means no foreground block at that offset. Otherwise the value is u + 2 c: used slot u of the device reached from this one by the offset's steps along the axes whose bits are set in c (bit 0 x, bit 1 y, bit 2 z); bits are set only on axes where the offset is nonzero, and c = 0 names this device. Unused slots hold -1 everywhere. Each device's blocks sit at distinct positions of its own region of 2 x 2 x 4 block positions, and the links follow that geometry. The most is reached in every draw.
All inputs are finite; a program needn't handle non-finite values.
Results may differ from the reference program's by a relative error of at most 0.0046.
Values may be sent and summed in bfloat16 or wider, within the bound.
A program may use at most 128 MiB of HBM per device.

```python
import jax
import jax.numpy as jnp
from jax import lax

CIN = 96
COUT = 48
EDGE = 16
VOX = 4096
SLOTS = 2
RX = 2
RY = 2
RZ = 4
N_GX = 4
N_GZ = 4
N_GY = 2


def permute_region(subkey):
    return jax.random.permutation(subkey, RX * RY * RZ)


def place_value(row, index, value):
    where_now = jnp.argmax((row == value).astype(jnp.int32)).astype(jnp.int32)
    current = row[index]
    return row.at[where_now].set(current).at[index].set(value)


def shared_layout(key):
    ndevices = N_GX * N_GZ * N_GY
    base = jax.random.fold_in(key, 4242)
    key_one, key_two, key_three, key_four = jax.random.split(base, 4)
    factor_one = jax.random.randint(key_one, (ndevices,), 0, SLOTS)
    factor_two = jax.random.randint(key_two, (ndevices,), 0, SLOTS)
    filled = 1 + factor_one * factor_two // max(SLOTS - 1, 1)
    chosen = jax.random.randint(key_three, (), 0, ndevices)
    corner_dev = (1 * N_GZ + 1) * N_GY + 1
    device_ids = jnp.arange(ndevices)
    filled = jnp.where((device_ids == chosen) | (device_ids == corner_dev), SLOTS, filled).astype(jnp.int32)
    ordering = jax.vmap(permute_region)(jax.random.split(key_four, ndevices)).astype(jnp.int32)
    first_row = place_value(ordering[0], 0, RX * RY * RZ - 1)
    ordering = ordering.at[0].set(first_row)
    corner_row = place_value(ordering[corner_dev], SLOTS - 1, 0)
    ordering = ordering.at[corner_dev].set(corner_row)
    inverse = jnp.argsort(ordering, axis=1).astype(jnp.int32)
    slot_of = jnp.where(inverse < filled[:, None], inverse, -1)
    device = jnp.arange(ndevices, dtype=jnp.int32)
    coord_y = jnp.broadcast_to((device % N_GY)[:, None], (ndevices, SLOTS))
    coord_z = jnp.broadcast_to((device // N_GY % N_GZ)[:, None], (ndevices, SLOTS))
    coord_x = jnp.broadcast_to((device // (N_GY * N_GZ))[:, None], (ndevices, SLOTS))
    position_id = ordering[:, :SLOTS]
    local_z = position_id % RZ
    local_y = position_id // RZ % RY
    local_x = position_id // (RZ * RY)
    used = jnp.arange(SLOTS)[None, :] < filled[:, None]
    region_sizes = [RX, RY, RZ]
    device_sizes = [N_GX, N_GY, N_GZ]
    columns = []
    for step_x in (-1, 0, 1):
        for step_y in (-1, 0, 1):
            for step_z in (-1, 0, 1):
                offsets = (step_x, step_y, step_z)
                if offsets == (0, 0, 0):
                    continue
                locals_now = [local_x, local_y, local_z]
                devices_now = [coord_x, coord_y, coord_z]
                present = used
                code = jnp.zeros_like(local_x)
                for axis_id in range(3):
                    if offsets[axis_id] == 0:
                        continue
                    stepped = locals_now[axis_id] + offsets[axis_id]
                    inside = (stepped >= 0) & (stepped < region_sizes[axis_id])
                    locals_now[axis_id] = stepped % region_sizes[axis_id]
                    devices_now[axis_id] = devices_now[axis_id] + jnp.where(inside, 0, offsets[axis_id])
                    code = code + jnp.where(inside, 0, 2 ** axis_id)
                    present = present & (devices_now[axis_id] >= 0) & (devices_now[axis_id] < device_sizes[axis_id])
                target_dev = (devices_now[0] * N_GZ + devices_now[2]) * N_GY + devices_now[1]
                target_dev = jnp.clip(target_dev, 0, ndevices - 1)
                target_pos = (locals_now[0] * RY + locals_now[1]) * RZ + locals_now[2]
                neighbour_slot = slot_of[target_dev, target_pos]
                encoded = jnp.where(present & (neighbour_slot >= 0), neighbour_slot + SLOTS * code, -1)
                columns.append(encoded)
    face_links = jnp.stack(columns, -1).astype(jnp.int32)
    return (filled.reshape(N_GX, N_GZ, N_GY), face_links.reshape(N_GX, N_GZ, N_GY * SLOTS, 26))


def draw_block_count(key, part):
    return shared_layout(key)[0]


def draw_neighbours(key, part):
    return shared_layout(key)[1]


def levels(key, extent, shards, smallest, largest):
    level = 1.0
    for axis_at, parts in shards:
        heights = jax.random.uniform(jax.random.fold_in(jax.random.fold_in(key, 6), axis_at), (parts,), jnp.float32, smallest / len(shards), largest / len(shards))
        level = level * jnp.repeat(jnp.exp(heights), extent[axis_at] // parts).reshape((-1,) + (1,) * (len(extent) - 1 - axis_at))
    return level


def centred(rng, dims, deviation, bound, shards=(), kind=jnp.bfloat16):
    drawn = jax.random.normal(rng, dims, jnp.float32) * deviation
    if len(shards) > 0:
        drawn = levels(rng, dims, shards, -0.22, 0.18) * drawn
    return jnp.clip(drawn, min=-bound, max=bound).astype(kind)


def setup_inputs(seed: int = 0) -> dict:
    streams_of = jax.random.split(jax.random.key(seed), 8)
    return {
        "blocks": centred(streams_of[0], (N_GX, N_GZ, N_GY * SLOTS, CIN, VOX), 1.0, 6.0, ((0, 4), (1, 4), (2, 2))),
        "block_count": draw_block_count(jax.random.fold_in(streams_of[7], 71), 0),
        "neighbours": draw_neighbours(jax.random.fold_in(streams_of[7], 71), 0),
        "conv_weight": centred(streams_of[3], (COUT, 27 * CIN), (27 * CIN) ** -0.5, 0.125),
        "conv_bias": centred(streams_of[4], (COUT,), 0.5, 3.0, (), jnp.float32),
        "head_weight": centred(streams_of[5], (COUT, COUT), COUT ** -0.5, 0.875),
        "head_bias": centred(streams_of[6], (COUT,), 0.5, 3.0, (), jnp.float32),
    }


def offset_list():
    return [(step_x, step_y, step_z) for step_x in (-1, 0, 1) for step_y in (-1, 0, 1) for step_z in (-1, 0, 1)]


def edge_piece(volume, offsets, first_axis):
    piece = volume
    for axis_id in range(3):
        dim = first_axis + axis_id
        length = piece.shape[dim]
        if offsets[axis_id] == -1:
            piece = lax.slice_in_dim(piece, length - 1, length, axis=dim)
        elif offsets[axis_id] == 1:
            piece = lax.slice_in_dim(piece, 0, 1, axis=dim)
    return piece


def assemble(pieces, first_axis):
    layers_x = []
    for step_x in (-1, 0, 1):
        layers_y = []
        for step_y in (-1, 0, 1):
            layers_y.append(jnp.concatenate([pieces[(step_x, step_y, step_z)] for step_z in (-1, 0, 1)], first_axis + 2))
        layers_x.append(jnp.concatenate(layers_y, first_axis + 1))
    return jnp.concatenate(layers_x, first_axis)


def convolve_padded(padded, conv_weight, conv_bias, head_weight, head_bias):
    channels = padded.shape[0]
    edge = padded.shape[1] - 2
    total = jnp.zeros((conv_weight.shape[0], edge * edge * edge), jnp.float32)
    for tap, offsets in enumerate(offset_list()):
        view = padded[:, 1 + offsets[0]:1 + offsets[0] + edge, 1 + offsets[1]:1 + offsets[1] + edge,
                      1 + offsets[2]:1 + offsets[2] + edge]
        total = total + jnp.dot(conv_weight[:, tap * channels:(tap + 1) * channels], view.reshape(channels, -1),
                                preferred_element_type=jnp.float32)
    hidden = jnp.maximum(total + conv_bias[:, None], 0.0).astype(jnp.bfloat16)
    mixed = jnp.dot(head_weight, hidden, preferred_element_type=jnp.float32) + head_bias[:, None]
    return mixed.astype(jnp.bfloat16)


def reference(blocks, block_count, neighbours, conv_weight, conv_bias, head_weight, head_bias):
    flat_blocks = blocks.reshape(-1, CIN, EDGE, EDGE, EDGE)
    face_links = neighbours.reshape(-1, 26)
    filled = block_count.reshape(-1)
    block_total = flat_blocks.shape[0]

    def compute_one(position):
        device = position // SLOTS
        slot_id = position % SLOTS
        coord_y = device % N_GY
        coord_z = (device // N_GY) % N_GZ
        coord_x = device // (N_GY * N_GZ)

        def active():
            volume = lax.dynamic_index_in_dim(flat_blocks, position, 0, keepdims=False)
            pieces = {(0, 0, 0): volume}
            link_index = 0
            for offsets in offset_list():
                if offsets == (0, 0, 0):
                    continue
                encoded = face_links[position, link_index]
                link_index += 1
                clean = jnp.maximum(encoded, 0)
                code = clean // SLOTS
                source_slot = clean % SLOTS
                target = [coord_x, coord_y, coord_z]
                for axis_id in range(3):
                    crossed = (code // (2 ** axis_id)) % 2
                    target[axis_id] = target[axis_id] + offsets[axis_id] * crossed
                source_dev = (target[0] * N_GZ + target[2]) * N_GY + target[1]
                source = jnp.clip(source_dev * SLOTS + source_slot, 0, block_total - 1).astype(jnp.int32)
                neighbour = lax.dynamic_index_in_dim(flat_blocks, source, 0, keepdims=False)
                face_piece = edge_piece(neighbour, offsets, 1)
                pieces[offsets] = jnp.where(encoded >= 0, face_piece, jnp.zeros_like(face_piece))
            padded = assemble(pieces, 1)
            return convolve_padded(padded, conv_weight, conv_bias, head_weight, head_bias)

        def vacant():
            return jnp.zeros((COUT, VOX), jnp.bfloat16)

        return lax.cond(slot_id < filled[device], active, vacant)

    results = lax.map(compute_one, jnp.arange(block_total, dtype=jnp.int32))
    return results.reshape(N_GX, N_GZ, N_GY * SLOTS, COUT, VOX)
```

```python
import functools

import jax
import jax.numpy as jnp
import numpy as np
from jax import lax
from jax.experimental import pallas as pl
from jax.experimental.pallas import tpu as pltpu
from jax.sharding import PartitionSpec as P

AXES = ("gx", "gy", "gz")
OFFSETS = [(a, b, c) for a in (-1, 0, 1) for b in (-1, 0, 1) for c in (-1, 0, 1)]
LINKS = [o for o in OFFSETS if o != (0, 0, 0)]
OWN = 27
ZERO = 33


def slot_of(e):
    return (e[0] + 1) * 9 + (e[1] + 1) * 3 + e[2] + 1


def last(step):
    return 0 if step == -1 else 1


def link_tables(slots):
    entry = np.zeros((26, 8), np.int32)
    base = np.zeros((26, 8), np.int32)
    slope = np.zeros((26, 8), np.int32)
    for i, o in enumerate(LINKS):
        for c in range(8):
            if any(c >> a & 1 and o[a] == 0 for a in range(3)):
                continue
            e = tuple(o[a] if c >> a & 1 else 0 for a in range(3))
            if c & 4:
                kind = "z"
            elif c & 1:
                kind = "x"
            elif c & 2:
                kind = "y"
            else:
                kind = "x" if o[0] else "y" if o[1] else "z"
            if c:
                entry[i, c] = slot_of(e) * slots
            else:
                axis = "xyz".index(kind)
                entry[i, c] = (OWN + 2 * axis + last(o[axis])) * slots
            source_x = {-1: 15, 0: 0, 1: 0}[o[0]]
            to_y = 15 if o[1] == 1 else 0
            to_z = 15 if o[2] == 1 else 0
            if kind == "x":
                base[i, c] = 240 * o[1] + 15 * o[2]
            elif kind == "y":
                base[i, c] = (to_y - source_x) * 16 + 15 * o[2]
                slope[i, c] = -16 if o[0] == 0 else 0
            else:
                base[i, c] = 240 * o[1] + to_z - source_x
                slope[i, c] = -1 if o[0] == 0 else 0
    return np.stack([entry, base % 256, slope]).reshape(3, 208)


def exchange_kernel(sizes, slots, blk, pool, send_sem, recv_sem):
    here = {axis: lax.axis_index(axis) for axis in AXES}

    def exists(d):
        ok = None
        for axis, step in zip(AXES, d):
            if step:
                at = here[axis] + step
                good = jnp.logical_and(at >= 0, at < sizes[axis])
                ok = good if ok is None else jnp.logical_and(ok, good)
        return ok

    def target(d):
        return {axis: here[axis] + step for axis, step in zip(AXES, d) if step}

    barrier = pltpu.get_barrier_semaphore()
    greet = 1
    for axis in AXES:
        inner = jnp.where(here[axis] > 0, 1, 0) + jnp.where(here[axis] < sizes[axis] - 1, 1, 0)
        greet = greet * (1 + inner)
    for d in LINKS:
        @pl.when(exists(d))
        def _():
            pl.semaphore_signal(
                barrier, inc=1, device_id=target(d), device_id_type=pl.DeviceIdType.MESH
            )
    pl.semaphore_wait(barrier, greet - 1)

    def copy_of(d):
        e = tuple(-step for step in d)
        at = slot_of(e)
        lanes = slice(0, 256)
        if d[1] and (d[0] or d[2]):
            lanes = slice(128, 256) if d[1] == 1 else slice(0, 128)
        if d[2]:
            src = pool.at[OWN + 4 + last(-d[2]), :, :, lanes]
        elif d[0]:
            start = 15 * 256 if d[0] == 1 else 0
            src = blk.at[:, :, start + lanes.start : start + lanes.stop]
        else:
            src = pool.at[OWN + 2 + last(-d[1])]
        return pltpu.make_async_remote_copy(
            src_ref=src,
            dst_ref=pool.at[at, :, :, lanes],
            send_sem=send_sem.at[at],
            recv_sem=recv_sem.at[at],
            device_id=target(d),
            device_id_type=pl.DeviceIdType.MESH,
        )

    def start(d):
        @pl.when(exists(d))
        def _():
            copy_of(d).start()

    for d in LINKS:
        if d[0] and not d[2]:
            start(d)

    lane = lax.broadcasted_iota(jnp.int32, (blk.shape[1], 128), 1)
    group, place = lane // 16, lane % 16

    def tile(u, x, half):
        at = x * 256 + half * 128
        return blk[u, :, at : at + 128].astype(jnp.float32)

    for side in (0, 1):
        for u in range(slots):
            for half in (0, 1):
                made = None
                for x in range(16):
                    shift = (x - 15) % 128 if side == 0 else x
                    moved = tile(u, x, half)
                    moved = pltpu.roll(moved, shift, 1) if shift else moved
                    made = moved if made is None else jnp.where(place == x, moved, made)
                pool[OWN + 4 + side, u, :, half * 128 : half * 128 + 128] = made.astype(pool.dtype)
    for d in LINKS:
        if d[2]:
            start(d)
    for side in (0, 1):
        for u in range(slots):
            for half in (0, 1):
                made = None
                for k in range(8):
                    x = half * 8 + k
                    shift = (k * 16 - 112) % 128 if side == 0 else k * 16
                    moved = tile(u, x, 1 - side)
                    moved = pltpu.roll(moved, shift, 1) if shift else moved
                    made = moved if made is None else jnp.where(group == k, moved, made)
                pool[OWN + 2 + side, u, :, half * 128 : half * 128 + 128] = made.astype(pool.dtype)
    for d in LINKS:
        if d[1] and not d[0] and not d[2]:
            start(d)
    for u in range(slots):
        pool[OWN, u] = blk[u, :, 15 * 256 : 16 * 256]
        pool[OWN + 1, u] = blk[u, :, 0:256]
        pool[ZERO, u] = jnp.zeros(pool.shape[2:], pool.dtype)
    for d in LINKS:
        @pl.when(exists(d))
        def _():
            copy_of(d).wait_send()
    for d in LINKS:
        e = tuple(-step for step in d)

        @pl.when(exists(e))
        def _():
            copy_of(d).wait_recv()


def conv_kernel(slots, count, links, table, blk, pool, w, cb, hw, hb, out, acc, stack):
    lane = lax.broadcasted_iota(jnp.int32, (blk.shape[1], 256), 1)
    row, col = lane // 16, lane % 16
    channels = blk.shape[1]
    cout = hw.shape[0]

    def roll(value, shift):
        if isinstance(shift, int):
            shift %= 256
            if shift == 0:
                return value
        return pltpu.roll(value, shift, 1)

    def fetch(s, o, x):
        i = LINKS.index(o)
        v = links[s, i]
        c = jnp.maximum(v, 0) // slots
        u = jnp.maximum(v, 0) % slots
        at = i * 8 + c
        entry = jnp.where(v < 0, ZERO * slots, table[0, at] + u)
        shift = lax.rem(table[1, at] + table[2, at] * x + 512, 256)
        return entry, shift

    def piece(s, o, x):
        entry, shift = fetch(s, o, x)
        return roll(pool[entry].astype(jnp.float32), shift)

    def plane(s, p, dx, centre):
        x = p - 1
        rows = {dy: piece(s, (dx, dy, 0), x) for dy in (-1, 1)}

        def put(dy, dz, value):
            t = (dy + 1) * 3 + dz + 1
            stack[t * channels : (t + 1) * channels, :] = value.astype(stack.dtype)

        for dz in (-1, 0, 1):
            if dz == 0:
                mid = centre
            else:
                edge = col == (0 if dz == -1 else 15)
                mid = jnp.where(edge, piece(s, (dx, 0, dz), x), roll(centre, -dz))
            put(0, dz, mid)
            for dy in (-1, 1):
                strip = rows[dy]
                if dz:
                    strip = jnp.where(edge, piece(s, (dx, dy, dz), x), roll(strip, -dz))
                put(dy, dz, jnp.where(row == (0 if dy == -1 else 15), strip, roll(mid, -16 * dy)))
        y = jnp.dot(w[...], stack[...], preferred_element_type=jnp.float32)
        for k in range(3):
            acc[p + 2 - k] += y[k * cout : (k + 1) * cout]

    def per_slot(s, _):
        acc[...] = jnp.zeros_like(acc)
        for p, dx in ((0, -1), (17, 1)):
            entry, _shift = fetch(s, (dx, 0, 0), 0)
            plane(s, p, dx, pool[entry].astype(jnp.float32))

        def inner(p, carry):
            at = pl.multiple_of((p - 1) * 256, 256)
            plane(s, p, 0, blk[s, :, pl.ds(at, 256)].astype(jnp.float32))
            return carry

        lax.fori_loop(1, 17, inner, 0)
        used = s < count[0]

        def finish(x, carry):
            hidden = jnp.maximum(acc[x + 2] + cb[...], 0.0).astype(jnp.bfloat16)
            mixed = jnp.dot(hw[...], hidden, preferred_element_type=jnp.float32) + hb[...]
            mixed = jnp.where(used, mixed, 0.0)
            out[s, :, pl.ds(pl.multiple_of(x * 256, 256), 256)] = mixed.astype(out.dtype)
            return carry

        lax.fori_loop(0, 16, finish, 0)
        return 0

    lax.fori_loop(0, slots, per_slot, 0)


def body(sizes, blocks, block_count, neighbours, conv_weight, conv_bias, head_weight, head_bias):
    slots, channels, voxels = blocks.shape[2:]
    cout = head_weight.shape[0]
    blk = blocks.reshape(slots, channels, voxels)
    vmem = pl.BlockSpec(memory_space=pltpu.VMEM)
    smem = pl.BlockSpec(memory_space=pltpu.SMEM)
    pool = pl.pallas_call(
        functools.partial(exchange_kernel, sizes, slots),
        out_shape=jax.ShapeDtypeStruct((ZERO + 1, slots, channels, 256), blocks.dtype),
        in_specs=[vmem],
        out_specs=vmem,
        scratch_shapes=[pltpu.SemaphoreType.DMA((27,)), pltpu.SemaphoreType.DMA((27,))],
        compiler_params=pltpu.CompilerParams(collective_id=0, has_side_effects=True),
        name="exchange",
    )(blk)
    taps = conv_weight.reshape(cout, 3, 9 * channels).transpose(1, 0, 2).reshape(3 * cout, 9 * channels)
    out = pl.pallas_call(
        functools.partial(conv_kernel, slots),
        out_shape=jax.ShapeDtypeStruct((slots, cout, voxels), jnp.bfloat16),
        in_specs=[smem] * 3 + [vmem] * 6,
        out_specs=vmem,
        scratch_shapes=[
            pltpu.VMEM((20, cout, 256), jnp.float32),
            pltpu.VMEM((9 * channels, 256), jnp.bfloat16),
        ],
        name="conv",
    )(
        block_count.reshape(1),
        neighbours.reshape(slots, 26),
        jnp.asarray(link_tables(slots)),
        blk,
        pool.reshape((ZERO + 1) * slots, channels, 256),
        taps,
        conv_bias[:, None],
        head_weight,
        head_bias[:, None],
    )
    return out.reshape(1, 1, slots, cout, voxels)


def solution(mesh):
    placed = (
        P("gx", "gz", "gy", None, None),
        P("gx", "gz", "gy"),
        P("gx", "gz", "gy", None),
        P(),
        P(),
        P(),
        P(),
    )
    return jax.shard_map(
        functools.partial(body, dict(mesh.shape)),
        mesh=mesh,
        in_specs=placed,
        out_specs=P("gx", "gz", "gy", None, None),
        check_vma=False,
    )
```

```python
import functools

import jax
import jax.numpy as jnp
import numpy as np
from jax import lax
from jax.experimental import pallas as pl
from jax.experimental.pallas import tpu as pltpu
from jax.sharding import PartitionSpec as P

AXES = ("gx", "gy", "gz")
OFFSETS = [(a, b, c) for a in (-1, 0, 1) for b in (-1, 0, 1) for c in (-1, 0, 1)]
LINKS = [o for o in OFFSETS if o != (0, 0, 0)]
OWN = 27
ZERO = 33


def slot_of(e):
    return (e[0] + 1) * 9 + (e[1] + 1) * 3 + e[2] + 1


def last(step):
    return 0 if step == -1 else 1


def link_tables(slots):
    entry = np.zeros((26, 8), np.int32)
    base = np.zeros((26, 8), np.int32)
    slope = np.zeros((26, 8), np.int32)
    for i, o in enumerate(LINKS):
        for c in range(8):
            if any(c >> a & 1 and o[a] == 0 for a in range(3)):
                continue
            e = tuple(o[a] if c >> a & 1 else 0 for a in range(3))
            if c & 4:
                kind = "z"
            elif c & 1:
                kind = "x"
            elif c & 2:
                kind = "y"
            else:
                kind = "x" if o[0] else "y" if o[1] else "z"
            if c:
                entry[i, c] = slot_of(e) * slots
            else:
                axis = "xyz".index(kind)
                entry[i, c] = (OWN + 2 * axis + last(o[axis])) * slots
            source_x = {-1: 15, 0: 0, 1: 0}[o[0]]
            to_y = 15 if o[1] == 1 else 0
            to_z = 15 if o[2] == 1 else 0
            if kind == "x":
                base[i, c] = 240 * o[1] + 15 * o[2]
            elif kind == "y":
                base[i, c] = (to_y - source_x) * 16 + 15 * o[2]
                slope[i, c] = -16 if o[0] == 0 else 0
            else:
                base[i, c] = 240 * o[1] + to_z - source_x
                slope[i, c] = -1 if o[0] == 0 else 0
    return np.stack([entry, base % 256, slope]).reshape(3, 208)


def exchange_kernel(sizes, slots, blk, pool, gone, came, send_sem, recv_sem):
    here = {axis: lax.axis_index(axis) for axis in AXES}

    def exists(d):
        ok = None
        for axis, step in zip(AXES, d):
            if step:
                at = here[axis] + step
                good = jnp.logical_and(at >= 0, at < sizes[axis])
                ok = good if ok is None else jnp.logical_and(ok, good)
        return ok

    def target(d):
        return {axis: here[axis] + step for axis, step in zip(AXES, d) if step}

    barrier = pltpu.get_barrier_semaphore()
    greet = 1
    for axis in AXES:
        inner = jnp.where(here[axis] > 0, 1, 0) + jnp.where(here[axis] < sizes[axis] - 1, 1, 0)
        greet = greet * (1 + inner)
    for d in LINKS:
        @pl.when(exists(d))
        def _():
            pl.semaphore_signal(
                barrier, inc=1, device_id=target(d), device_id_type=pl.DeviceIdType.MESH
            )
    pl.semaphore_wait(barrier, greet - 1)

    lane = lax.broadcasted_iota(jnp.int32, (blk.shape[1], 128), 1)
    group, place = lane // 16, lane % 16

    def roll(value, shift):
        shift %= 128
        return pltpu.roll(value, shift, 1) if shift else value

    def end_lanes(step):
        return slice(128, 256) if step == 1 else slice(0, 128)

    def packed(d):
        if d[1] and d[2]:
            return 8 + (d[1] + 1) + (d[2] + 1) // 2
        if d[1]:
            return (d[0] + 1) + (d[1] + 1) // 2
        return 4 + (d[0] + 1) + (d[2] + 1) // 2

    def copy_of(d):
        at = slot_of(tuple(-step for step in d))
        dst = pool.at[at]
        if sum(map(abs, d)) > 1:
            src, dst = gone.at[packed(d)], came.at[at]
        elif d[0]:
            src = blk.at[:, :, (15 * 256 if d[0] == 1 else 0) : (16 * 256 if d[0] == 1 else 256)]
        else:
            src = pool.at[OWN + (2 if d[1] else 4) + last(-d[1] - d[2])]
        return pltpu.make_async_remote_copy(
            src_ref=src,
            dst_ref=dst,
            send_sem=send_sem.at[at],
            recv_sem=recv_sem.at[at],
            device_id=target(d),
            device_id_type=pl.DeviceIdType.MESH,
        )

    def start(d):
        @pl.when(exists(d))
        def _():
            copy_of(d).start()

    def end_row(d, first, second):
        keep = group == (7 if d[1] == 1 else 0)
        return jnp.where(keep, first, roll(second, 64))

    start((1, 0, 0))
    start((-1, 0, 0))

    def tile(u, x, half):
        at = x * 256 + half * 128
        return blk[u, :, at : at + 128]

    for d in LINKS:
        if d[0] and d[1] and not d[2]:
            x, half = (15 if d[0] == 1 else 0), (1 if d[1] == 1 else 0)
            gone[packed(d)] = end_row(d, tile(0, x, half), tile(1, x, half))
            start(d)
    for dz in (1, -1):
        side = last(-dz)
        faces = {}
        for u in range(slots):
            for half in (0, 1):
                made = None
                for x in range(16):
                    moved = roll(tile(u, x, half), x - 15 if side == 0 else x)
                    made = moved if made is None else jnp.where(place == x, moved, made)
                pool[OWN + 4 + side, u, :, half * 128 : half * 128 + 128] = made
                faces[u, half] = made
        start((0, 0, dz))
        for dx in (1, -1):
            d = (dx, 0, dz)
            made = None
            for u in range(slots):
                for half in (0, 1):
                    moved = roll(faces[u, half], 2 * u + half - (15 if dx == 1 else 0))
                    made = moved if made is None else jnp.where(place == 2 * u + half, moved, made)
            gone[packed(d)] = made
            start(d)
        for dy in (1, -1):
            d = (0, dy, dz)
            half = 1 if dy == 1 else 0
            gone[packed(d)] = end_row(d, faces[0, half], faces[1, half])
            for dx in (0, 1, -1):
                start((dx, dy, dz))
    for side in (0, 1):
        for u in range(slots):
            for half in (0, 1):
                made = None
                for k in range(8):
                    moved = roll(tile(u, half * 8 + k, 1 - side), k * 16 - (112 if side == 0 else 0))
                    made = moved if made is None else jnp.where(group == k, moved, made)
                pool[OWN + 2 + side, u, :, half * 128 : half * 128 + 128] = made
        start((0, 1 if side == 0 else -1, 0))
    for u in range(slots):
        pool[OWN, u] = blk[u, :, 15 * 256 : 16 * 256]
        pool[OWN + 1, u] = blk[u, :, 0:256]
        pool[ZERO, u] = jnp.zeros(pool.shape[2:], pool.dtype)
    for d in LINKS:
        e = tuple(-step for step in d)
        at = slot_of(e)

        @pl.when(exists(e))
        def _():
            copy_of(d).wait_recv()
            if sum(map(abs, d)) == 1:
                return
            message = came[at]
            if d[1]:
                for u in range(slots):
                    pool[at, u, :, end_lanes(d[1])] = roll(message, 64 * u)
            else:
                for u in range(slots):
                    for half in (0, 1):
                        back = (15 if d[0] == 1 else 0) - 2 * u - half
                        pool[at, u, :, half * 128 : half * 128 + 128] = roll(message, back)
    for d in LINKS:
        @pl.when(exists(d))
        def _():
            copy_of(d).wait_send()


def conv_kernel(slots, count, links, table, blk, pool, cw, cb, hw, hb, out, w, acc, even, odd):
    channels = blk.shape[1]
    cout = hw.shape[0]
    lane = lax.broadcasted_iota(jnp.int32, (channels, 256), 1)
    row, col = lane // 16, lane % 16
    eye = lax.broadcasted_iota(jnp.int32, (cout, cout), 0) == lax.broadcasted_iota(
        jnp.int32, (cout, cout), 1
    )

    def column(ref):
        return jnp.sum(jnp.where(eye, ref[...], 0.0), axis=1, keepdims=True)

    bias, head_bias = column(cb), column(hb)
    depth = 9 * channels
    for k in range(3):
        w[k * cout : (k + 1) * cout, :] = cw[:, k * depth : (k + 1) * depth]

    def fetch(s, o, x):
        i = LINKS.index(o)
        v = links[s, i]
        c = jnp.maximum(v, 0) // slots
        u = jnp.maximum(v, 0) % slots
        at = i * 8 + c
        entry = jnp.where(v < 0, ZERO * slots, table[0, at] + u)
        shift = lax.rem(table[1, at] + table[2, at] * x + 512, 256)
        return entry, shift

    def part(s, o, x):
        entry, shift = fetch(s, o, x)
        lands = (15 if o[1] == 1 else 0) * 16 + (15 if o[2] == 1 else 0)
        half = lax.rem(lands - shift + 256, 256) // 128
        got = pool[entry, :, pl.ds(pl.multiple_of(half * 128, 128), 128)]
        return pltpu.roll(got, lax.rem(shift, 128), 1)

    def build(stack, s, p, dx, centre):
        x = p - 1
        rows = {dy: part(s, (dx, dy, 0), x) for dy in (-1, 1)}
        for dz in (-1, 0, 1):
            mid = centre
            if dz:
                edge = col == (0 if dz == -1 else 15)
                entry, shift = fetch(s, (dx, 0, dz), x)
                mid = jnp.where(edge, pltpu.roll(pool[entry], shift, 1), pltpu.roll(centre, -dz % 256, 1))
            for dy in (-1, 0, 1):
                t = ((dy + 1) * 3 + dz + 1) * channels
                if dy == 0:
                    stack[t : t + channels, :] = mid
                    continue
                moved = pltpu.roll(mid, -16 * dy % 256, 1)
                strip = rows[dy]
                lanes = slice(0, 128) if dy == -1 else slice(128, 256)
                if dz:
                    strip = jnp.where(
                        edge[:, lanes], part(s, (dx, dy, dz), x), pltpu.roll(strip, -dz % 128, 1)
                    )
                other = slice(128, 256) if dy == -1 else slice(0, 128)
                stack[t : t + channels, other] = moved[:, other]
                stack[t : t + channels, lanes] = jnp.where(
                    row[:, lanes] == (0 if dy == -1 else 15), strip, moved[:, lanes]
                )

    def multiply(stack, p):
        y = jnp.dot(w[...], stack[...], preferred_element_type=jnp.float32)
        for k in range(3):
            acc[p + 2 - k] += y[k * cout : (k + 1) * cout]

    def per_slot(s, _):
        acc[...] = jnp.zeros_like(acc)

        def shell(stack, p, dx):
            entry, _shift = fetch(s, (dx, 0, 0), 0)
            build(stack, s, p, dx, pool[entry])

        def inside(stack, p):
            at = pl.multiple_of((p - 1) * 256, 256)
            build(stack, s, p, 0, blk[s, :, pl.ds(at, 256)])

        shell(even, 0, -1)

        def inner(k, carry):
            inside(odd, 2 * k + 1)
            multiply(even, 2 * k)
            inside(even, 2 * k + 2)
            multiply(odd, 2 * k + 1)
            return carry

        lax.fori_loop(0, 8, inner, 0)
        shell(odd, 17, 1)
        multiply(even, 16)
        multiply(odd, 17)
        used = s < count[0]

        def finish(x, carry):
            hidden = jnp.maximum(acc[x + 2] + bias, 0.0).astype(jnp.bfloat16)
            mixed = jnp.dot(hw[...], hidden, preferred_element_type=jnp.float32) + head_bias
            mixed = jnp.where(used, mixed, 0.0)
            out[s, :, pl.ds(pl.multiple_of(x * 256, 256), 256)] = mixed.astype(out.dtype)
            return carry

        lax.fori_loop(0, 16, finish, 0, unroll=4)
        return 0

    lax.fori_loop(0, slots, per_slot, 0)


def body(sizes, blocks, block_count, neighbours, conv_weight, conv_bias, head_weight, head_bias):
    slots, channels, voxels = blocks.shape[2:]
    cout = head_weight.shape[0]
    blk = blocks.reshape(slots, channels, voxels)
    vmem = pl.BlockSpec(memory_space=pltpu.VMEM)
    smem = pl.BlockSpec(memory_space=pltpu.SMEM)
    pool = pl.pallas_call(
        functools.partial(exchange_kernel, sizes, slots),
        out_shape=jax.ShapeDtypeStruct((ZERO + 1, slots, channels, 256), blocks.dtype),
        in_specs=[vmem],
        out_specs=vmem,
        scratch_shapes=[
            pltpu.VMEM((12, channels, 128), blocks.dtype),
            pltpu.VMEM((27, channels, 128), blocks.dtype),
            pltpu.SemaphoreType.DMA((27,)),
            pltpu.SemaphoreType.DMA((27,)),
        ],
        compiler_params=pltpu.CompilerParams(collective_id=0, has_side_effects=True),
        name="exchange",
    )(blk)
    out = pl.pallas_call(
        functools.partial(conv_kernel, slots),
        out_shape=jax.ShapeDtypeStruct((slots, cout, voxels), jnp.bfloat16),
        in_specs=[smem] * 3 + [vmem] * 6,
        out_specs=vmem,
        scratch_shapes=[
            pltpu.VMEM((3 * cout, 9 * channels), jnp.bfloat16),
            pltpu.VMEM((20, cout, 256), jnp.float32),
            pltpu.VMEM((9 * channels, 256), jnp.bfloat16),
            pltpu.VMEM((9 * channels, 256), jnp.bfloat16),
        ],
        name="conv",
    )(
        block_count.reshape(1),
        neighbours.reshape(slots, 26),
        jnp.asarray(link_tables(slots)),
        blk,
        pool.reshape((ZERO + 1) * slots, channels, 256),
        conv_weight,
        conv_bias[None],
        head_weight,
        head_bias[None],
    )
    return out.reshape(1, 1, slots, cout, voxels)


def solution(mesh):
    placed = (
        P("gx", "gz", "gy", None, None),
        P("gx", "gz", "gy"),
        P("gx", "gz", "gy", None),
        P(),
        P(),
        P(),
        P(),
    )
    return jax.shard_map(
        functools.partial(body, dict(mesh.shape)),
        mesh=mesh,
        in_specs=placed,
        out_specs=P("gx", "gz", "gy", None, None),
        check_vma=False,
    )
```

```python
import functools

import jax
import jax.numpy as jnp
import numpy as np
from jax import lax
from jax.experimental import pallas as pl
from jax.experimental.pallas import tpu as pltpu
from jax.sharding import PartitionSpec as P

AXES = ("gx", "gy", "gz")
OFFSETS = [(a, b, c) for a in (-1, 0, 1) for b in (-1, 0, 1) for c in (-1, 0, 1)]
LINKS = [o for o in OFFSETS if o != (0, 0, 0)]
OWN = 27
ZERO = 33


def slot_of(e):
    return (e[0] + 1) * 9 + (e[1] + 1) * 3 + e[2] + 1


def last(step):
    return 0 if step == -1 else 1


def link_tables(slots):
    entry = np.zeros((26, 8), np.int32)
    base = np.zeros((26, 8), np.int32)
    slope = np.zeros((26, 8), np.int32)
    for i, o in enumerate(LINKS):
        for c in range(8):
            if any(c >> a & 1 and o[a] == 0 for a in range(3)):
                continue
            e = tuple(o[a] if c >> a & 1 else 0 for a in range(3))
            if c & 4:
                kind = "z"
            elif c & 1:
                kind = "x"
            elif c & 2:
                kind = "y"
            else:
                kind = "x" if o[0] else "y" if o[1] else "z"
            if c:
                entry[i, c] = slot_of(e) * slots
            else:
                axis = "xyz".index(kind)
                entry[i, c] = (OWN + 2 * axis + last(o[axis])) * slots
            source_x = {-1: 15, 0: 0, 1: 0}[o[0]]
            to_y = 15 if o[1] == 1 else 0
            to_z = 15 if o[2] == 1 else 0
            if kind == "x":
                base[i, c] = 240 * o[1] + 15 * o[2]
            elif kind == "y":
                base[i, c] = (to_y - source_x) * 16 + 15 * o[2]
                slope[i, c] = -16 if o[0] == 0 else 0
            else:
                base[i, c] = 240 * o[1] + to_z - source_x
                slope[i, c] = -1 if o[0] == 0 else 0
    return np.stack([entry, base % 256, slope]).reshape(3, 208)


def exchange_kernel(sizes, slots, blk, pool, gone, came, send_sem, recv_sem):
    here = {axis: lax.axis_index(axis) for axis in AXES}

    def exists(d):
        ok = None
        for axis, step in zip(AXES, d):
            if step:
                at = here[axis] + step
                good = jnp.logical_and(at >= 0, at < sizes[axis])
                ok = good if ok is None else jnp.logical_and(ok, good)
        return ok

    def target(d):
        return {axis: here[axis] + step for axis, step in zip(AXES, d) if step}

    barrier = pltpu.get_barrier_semaphore()
    greet = 1
    for axis in AXES:
        inner = jnp.where(here[axis] > 0, 1, 0) + jnp.where(here[axis] < sizes[axis] - 1, 1, 0)
        greet = greet * (1 + inner)
    for d in LINKS:
        @pl.when(exists(d))
        def _():
            pl.semaphore_signal(
                barrier, inc=1, device_id=target(d), device_id_type=pl.DeviceIdType.MESH
            )
    lane = lax.broadcasted_iota(jnp.int32, (blk.shape[1], 128), 1)
    group, place = lane // 16, lane % 16

    def roll(value, shift):
        shift %= 128
        return pltpu.roll(value, shift, 1) if shift else value

    def end_lanes(step):
        return slice(128, 256) if step == 1 else slice(0, 128)

    def packed(d):
        if d[1] and d[2]:
            return 8 + (d[1] + 1) + (d[2] + 1) // 2
        if d[1]:
            return (d[0] + 1) + (d[1] + 1) // 2
        return 4 + (d[0] + 1) + (d[2] + 1) // 2

    def copy_of(d):
        at = slot_of(tuple(-step for step in d))
        dst = pool.at[at]
        if sum(map(abs, d)) > 1:
            src, dst = gone.at[packed(d)], came.at[at]
        elif d[0]:
            src = blk.at[:, :, (15 * 256 if d[0] == 1 else 0) : (16 * 256 if d[0] == 1 else 256)]
        else:
            src = pool.at[OWN + (2 if d[1] else 4) + last(-d[1] - d[2])]
        return pltpu.make_async_remote_copy(
            src_ref=src,
            dst_ref=dst,
            send_sem=send_sem.at[at],
            recv_sem=recv_sem.at[at],
            device_id=target(d),
            device_id_type=pl.DeviceIdType.MESH,
        )

    def start(d):
        @pl.when(exists(d))
        def _():
            copy_of(d).start()

    def end_row(d, first, second):
        keep = group == (7 if d[1] == 1 else 0)
        return jnp.where(keep, first, roll(second, 64))

    def tile(u, x, half):
        at = x * 256 + half * 128
        return blk[u, :, at : at + 128]

    for d in LINKS:
        if d[0] and d[1] and not d[2]:
            x, half = (15 if d[0] == 1 else 0), (1 if d[1] == 1 else 0)
            gone[packed(d)] = end_row(d, tile(0, x, half), tile(1, x, half))
    for dz in (1, -1):
        side = last(-dz)
        faces = {}
        for u in range(slots):
            for half in (0, 1):
                made = None
                for x in range(16):
                    moved = roll(tile(u, x, half), x - 15 if side == 0 else x)
                    made = moved if made is None else jnp.where(place == x, moved, made)
                pool[OWN + 4 + side, u, :, half * 128 : half * 128 + 128] = made
                faces[u, half] = made
        for dx in (1, -1):
            d = (dx, 0, dz)
            made = None
            for u in range(slots):
                for half in (0, 1):
                    moved = roll(faces[u, half], 2 * u + half - (15 if dx == 1 else 0))
                    made = moved if made is None else jnp.where(place == 2 * u + half, moved, made)
            gone[packed(d)] = made
        for dy in (1, -1):
            d = (0, dy, dz)
            half = 1 if dy == 1 else 0
            gone[packed(d)] = end_row(d, faces[0, half], faces[1, half])
    for side in (0, 1):
        for u in range(slots):
            for half in (0, 1):
                made = None
                for k in range(8):
                    moved = roll(tile(u, half * 8 + k, 1 - side), k * 16 - (112 if side == 0 else 0))
                    made = moved if made is None else jnp.where(group == k, moved, made)
                pool[OWN + 2 + side, u, :, half * 128 : half * 128 + 128] = made
    pl.semaphore_wait(barrier, greet - 1)
    for d in sorted(LINKS, key=lambda d: (sum(map(abs, d)), -abs(d[0]))):
        start(d)
    for u in range(slots):
        pool[OWN, u] = blk[u, :, 15 * 256 : 16 * 256]
        pool[OWN + 1, u] = blk[u, :, 0:256]
        pool[ZERO, u] = jnp.zeros(pool.shape[2:], pool.dtype)
    for d in LINKS:
        e = tuple(-step for step in d)
        at = slot_of(e)

        @pl.when(exists(e))
        def _():
            copy_of(d).wait_recv()
            if sum(map(abs, d)) == 1:
                return
            message = came[at]
            if d[1]:
                for u in range(slots):
                    pool[at, u, :, end_lanes(d[1])] = roll(message, 64 * u)
            else:
                for u in range(slots):
                    for half in (0, 1):
                        back = (15 if d[0] == 1 else 0) - 2 * u - half
                        pool[at, u, :, half * 128 : half * 128 + 128] = roll(message, back)
    for d in LINKS:
        @pl.when(exists(d))
        def _():
            copy_of(d).wait_send()


def conv_kernel(slots, count, links, table, blk, pool, cw, cb, hw, hb, out, w, acc, even, odd):
    channels = blk.shape[1]
    cout = hw.shape[0]
    lane = lax.broadcasted_iota(jnp.int32, (channels, 256), 1)
    row, col = lane // 16, lane % 16
    eye = lax.broadcasted_iota(jnp.int32, (cout, cout), 0) == lax.broadcasted_iota(
        jnp.int32, (cout, cout), 1
    )

    def column(ref):
        return jnp.sum(jnp.where(eye, ref[...], 0.0), axis=1, keepdims=True)

    bias, head_bias = column(cb), column(hb)
    depth = 9 * channels
    for k in range(3):
        w[k * cout : (k + 1) * cout, :] = cw[:, k * depth : (k + 1) * depth]

    def fetch(s, o, x):
        i = LINKS.index(o)
        v = links[s, i]
        c = jnp.maximum(v, 0) // slots
        u = jnp.maximum(v, 0) % slots
        at = i * 8 + c
        entry = jnp.where(v < 0, ZERO * slots, table[0, at] + u)
        shift = lax.rem(table[1, at] + table[2, at] * x + 512, 256)
        return entry, shift

    def part(s, o, x):
        entry, shift = fetch(s, o, x)
        lands = (15 if o[1] == 1 else 0) * 16 + (15 if o[2] == 1 else 0)
        half = lax.rem(lands - shift + 256, 256) // 128
        got = pool[entry, :, pl.ds(pl.multiple_of(half * 128, 128), 128)]
        return pltpu.roll(got, lax.rem(shift, 128), 1)

    def build(stack, s, p, dx, centre):
        x = p - 1
        rows = {dy: part(s, (dx, dy, 0), x) for dy in (-1, 1)}
        for dz in (-1, 0, 1):
            mid = centre
            if dz:
                edge = col == (0 if dz == -1 else 15)
                entry, shift = fetch(s, (dx, 0, dz), x)
                mid = jnp.where(edge, pltpu.roll(pool[entry], shift, 1), pltpu.roll(centre, -dz % 256, 1))
            for dy in (-1, 0, 1):
                t = ((dy + 1) * 3 + dz + 1) * channels
                if dy == 0:
                    stack[t : t + channels, :] = mid
                    continue
                moved = pltpu.roll(mid, -16 * dy % 256, 1)
                strip = rows[dy]
                lanes = slice(0, 128) if dy == -1 else slice(128, 256)
                if dz:
                    strip = jnp.where(
                        edge[:, lanes], part(s, (dx, dy, dz), x), pltpu.roll(strip, -dz % 128, 1)
                    )
                other = slice(128, 256) if dy == -1 else slice(0, 128)
                stack[t : t + channels, other] = moved[:, other]
                stack[t : t + channels, lanes] = jnp.where(
                    row[:, lanes] == (0 if dy == -1 else 15), strip, moved[:, lanes]
                )

    def multiply(stack, p):
        y = jnp.dot(w[...], stack[...], preferred_element_type=jnp.float32)
        for k in range(3):
            acc[p + 2 - k] += y[k * cout : (k + 1) * cout]

    def per_slot(s, _):
        acc[...] = jnp.zeros_like(acc)

        def shell(stack, p, dx):
            entry, _shift = fetch(s, (dx, 0, 0), 0)
            build(stack, s, p, dx, pool[entry])

        def inside(stack, p):
            at = pl.multiple_of((p - 1) * 256, 256)
            build(stack, s, p, 0, blk[s, :, pl.ds(at, 256)])

        shell(even, 0, -1)

        def inner(k, carry):
            inside(odd, 2 * k + 1)
            multiply(even, 2 * k)
            inside(even, 2 * k + 2)
            multiply(odd, 2 * k + 1)
            return carry

        lax.fori_loop(0, 8, inner, 0)
        shell(odd, 17, 1)
        multiply(even, 16)
        multiply(odd, 17)
        used = s < count[0]

        def finish(x, carry):
            hidden = jnp.maximum(acc[x + 2] + bias, 0.0).astype(jnp.bfloat16)
            mixed = jnp.dot(hw[...], hidden, preferred_element_type=jnp.float32) + head_bias
            mixed = jnp.where(used, mixed, 0.0)
            out[s, :, pl.ds(pl.multiple_of(x * 256, 256), 256)] = mixed.astype(out.dtype)
            return carry

        lax.fori_loop(0, 16, finish, 0, unroll=4)
        return 0

    lax.fori_loop(0, slots, per_slot, 0)


def body(sizes, blocks, block_count, neighbours, conv_weight, conv_bias, head_weight, head_bias):
    slots, channels, voxels = blocks.shape[2:]
    cout = head_weight.shape[0]
    blk = blocks.reshape(slots, channels, voxels)
    vmem = pl.BlockSpec(memory_space=pltpu.VMEM)
    smem = pl.BlockSpec(memory_space=pltpu.SMEM)
    pool = pl.pallas_call(
        functools.partial(exchange_kernel, sizes, slots),
        out_shape=jax.ShapeDtypeStruct((ZERO + 1, slots, channels, 256), blocks.dtype),
        in_specs=[vmem],
        out_specs=vmem,
        scratch_shapes=[
            pltpu.VMEM((12, channels, 128), blocks.dtype),
            pltpu.VMEM((27, channels, 128), blocks.dtype),
            pltpu.SemaphoreType.DMA((27,)),
            pltpu.SemaphoreType.DMA((27,)),
        ],
        compiler_params=pltpu.CompilerParams(collective_id=0, has_side_effects=True),
        name="exchange",
    )(blk)
    out = pl.pallas_call(
        functools.partial(conv_kernel, slots),
        out_shape=jax.ShapeDtypeStruct((slots, cout, voxels), jnp.bfloat16),
        in_specs=[smem] * 3 + [vmem] * 6,
        out_specs=vmem,
        scratch_shapes=[
            pltpu.VMEM((3 * cout, 9 * channels), jnp.bfloat16),
            pltpu.VMEM((20, cout, 256), jnp.float32),
            pltpu.VMEM((9 * channels, 256), jnp.bfloat16),
            pltpu.VMEM((9 * channels, 256), jnp.bfloat16),
        ],
        name="conv",
    )(
        block_count.reshape(1),
        neighbours.reshape(slots, 26),
        jnp.asarray(link_tables(slots)),
        blk,
        pool.reshape((ZERO + 1) * slots, channels, 256),
        conv_weight,
        conv_bias[None],
        head_weight,
        head_bias[None],
    )
    return out.reshape(1, 1, slots, cout, voxels)


def solution(mesh):
    placed = (
        P("gx", "gz", "gy", None, None),
        P("gx", "gz", "gy"),
        P("gx", "gz", "gy", None),
        P(),
        P(),
        P(),
        P(),
    )
    return jax.shard_map(
        functools.partial(body, dict(mesh.shape)),
        mesh=mesh,
        in_specs=placed,
        out_specs=P("gx", "gz", "gy", None, None),
        check_vma=False,
    )
```

```python
import functools

import jax
import jax.numpy as jnp
import numpy as np
from jax import lax
from jax.experimental import pallas as pl
from jax.experimental.pallas import tpu as pltpu
from jax.sharding import PartitionSpec as P

AXES = ("gx", "gy", "gz")
OFFSETS = [(a, b, c) for a in (-1, 0, 1) for b in (-1, 0, 1) for c in (-1, 0, 1)]
LINKS = [o for o in OFFSETS if o != (0, 0, 0)]
OWN = 27
ZERO = 33


def slot_of(e):
    return (e[0] + 1) * 9 + (e[1] + 1) * 3 + e[2] + 1


def last(step):
    return 0 if step == -1 else 1


def link_tables(slots):
    entry = np.zeros((26, 8), np.int32)
    base = np.zeros((26, 8), np.int32)
    slope = np.zeros((26, 8), np.int32)
    for i, o in enumerate(LINKS):
        for c in range(8):
            if any(c >> a & 1 and o[a] == 0 for a in range(3)):
                continue
            e = tuple(o[a] if c >> a & 1 else 0 for a in range(3))
            if c & 4:
                kind = "z"
            elif c & 1:
                kind = "x"
            elif c & 2:
                kind = "y"
            else:
                kind = "x" if o[0] else "y" if o[1] else "z"
            if c:
                entry[i, c] = slot_of(e) * slots
            else:
                axis = "xyz".index(kind)
                entry[i, c] = (OWN + 2 * axis + last(o[axis])) * slots
            source_x = {-1: 15, 0: 0, 1: 0}[o[0]]
            to_y = 15 if o[1] == 1 else 0
            to_z = 15 if o[2] == 1 else 0
            if kind == "x":
                base[i, c] = 240 * o[1] + 15 * o[2]
            elif kind == "y":
                base[i, c] = (to_y - source_x) * 16 + 15 * o[2]
                slope[i, c] = -16 if o[0] == 0 else 0
            else:
                base[i, c] = 240 * o[1] + to_z - source_x
                slope[i, c] = -1 if o[0] == 0 else 0
    return np.stack([entry, base % 256, slope]).reshape(3, 208)


def exchange_kernel(sizes, slots, blk, pool, gone, came, send_sem, recv_sem):
    here = {axis: lax.axis_index(axis) for axis in AXES}

    def exists(d):
        ok = None
        for axis, step in zip(AXES, d):
            if step:
                at = here[axis] + step
                good = jnp.logical_and(at >= 0, at < sizes[axis])
                ok = good if ok is None else jnp.logical_and(ok, good)
        return ok

    def target(d):
        return {axis: here[axis] + step for axis, step in zip(AXES, d) if step}

    barrier = pltpu.get_barrier_semaphore()
    greet = 1
    for axis in AXES:
        inner = jnp.where(here[axis] > 0, 1, 0) + jnp.where(here[axis] < sizes[axis] - 1, 1, 0)
        greet = greet * (1 + inner)
    for d in LINKS:
        @pl.when(exists(d))
        def _():
            pl.semaphore_signal(
                barrier, inc=1, device_id=target(d), device_id_type=pl.DeviceIdType.MESH
            )
    lane = lax.broadcasted_iota(jnp.int32, (blk.shape[1], 128), 1)
    group, place = lane // 16, lane % 16

    def roll(value, shift):
        shift %= 128
        return pltpu.roll(value, shift, 1) if shift else value

    def end_lanes(step):
        return slice(128, 256) if step == 1 else slice(0, 128)

    def packed(d):
        if d[1] and d[2]:
            return 8 + (d[1] + 1) + (d[2] + 1) // 2
        if d[1]:
            return (d[0] + 1) + (d[1] + 1) // 2
        return 4 + (d[0] + 1) + (d[2] + 1) // 2

    def copy_of(d):
        at = slot_of(tuple(-step for step in d))
        dst = pool.at[at]
        if sum(map(abs, d)) > 1:
            src, dst = gone.at[packed(d)], came.at[at]
        elif d[0]:
            src = blk.at[:, :, (15 * 256 if d[0] == 1 else 0) : (16 * 256 if d[0] == 1 else 256)]
        else:
            src = pool.at[OWN + (2 if d[1] else 4) + last(-d[1] - d[2])]
        return pltpu.make_async_remote_copy(
            src_ref=src,
            dst_ref=dst,
            send_sem=send_sem.at[at],
            recv_sem=recv_sem.at[at],
            device_id=target(d),
            device_id_type=pl.DeviceIdType.MESH,
        )

    def start(d):
        @pl.when(exists(d))
        def _():
            copy_of(d).start()

    def end_row(d, first, second):
        keep = group == (7 if d[1] == 1 else 0)
        return jnp.where(keep, first, roll(second, 64))

    def tile(u, x, half):
        at = x * 256 + half * 128
        return blk[u, :, at : at + 128]

    for d in LINKS:
        if d[0] and d[1] and not d[2]:
            x, half = (15 if d[0] == 1 else 0), (1 if d[1] == 1 else 0)
            gone[packed(d)] = end_row(d, tile(0, x, half), tile(1, x, half))
    for dz in (1, -1):
        side = last(-dz)
        faces = {}
        for u in range(slots):
            for half in (0, 1):
                made = None
                for x in range(16):
                    moved = roll(tile(u, x, half), x - 15 if side == 0 else x)
                    made = moved if made is None else jnp.where(place == x, moved, made)
                pool[OWN + 4 + side, u, :, half * 128 : half * 128 + 128] = made
                faces[u, half] = made
        for dx in (1, -1):
            d = (dx, 0, dz)
            made = None
            for u in range(slots):
                for half in (0, 1):
                    moved = roll(faces[u, half], 2 * u + half - (15 if dx == 1 else 0))
                    made = moved if made is None else jnp.where(place == 2 * u + half, moved, made)
            gone[packed(d)] = made
        for dy in (1, -1):
            d = (0, dy, dz)
            half = 1 if dy == 1 else 0
            gone[packed(d)] = end_row(d, faces[0, half], faces[1, half])
    for side in (0, 1):
        for u in range(slots):
            for half in (0, 1):
                made = None
                for k in range(8):
                    moved = roll(tile(u, half * 8 + k, 1 - side), k * 16 - (112 if side == 0 else 0))
                    made = moved if made is None else jnp.where(group == k, moved, made)
                pool[OWN + 2 + side, u, :, half * 128 : half * 128 + 128] = made
    pl.semaphore_wait(barrier, greet - 1)
    for d in sorted(LINKS, key=lambda d: (sum(map(abs, d)), -abs(d[0]))):
        start(d)
    for u in range(slots):
        pool[OWN, u] = blk[u, :, 15 * 256 : 16 * 256]
        pool[OWN + 1, u] = blk[u, :, 0:256]
        pool[ZERO, u] = jnp.zeros(pool.shape[2:], pool.dtype)
    for d in LINKS:
        e = tuple(-step for step in d)
        at = slot_of(e)

        @pl.when(exists(e))
        def _():
            copy_of(d).wait_recv()
            if sum(map(abs, d)) == 1:
                return
            message = came[at]
            if d[1]:
                for u in range(slots):
                    pool[at, u, :, end_lanes(d[1])] = roll(message, 64 * u)
            else:
                for u in range(slots):
                    for half in (0, 1):
                        back = (15 if d[0] == 1 else 0) - 2 * u - half
                        pool[at, u, :, half * 128 : half * 128 + 128] = roll(message, back)
    for d in LINKS:
        @pl.when(exists(d))
        def _():
            copy_of(d).wait_send()


def conv_kernel(slots, count, links, table, blk, pool, cw, cb, hw, hb, out, w, acc, even, odd):
    channels = blk.shape[1]
    cout = hw.shape[0]
    lane = lax.broadcasted_iota(jnp.int32, (channels, 256), 1)
    row, col = lane // 16, lane % 16
    eye = lax.broadcasted_iota(jnp.int32, (cout, cout), 0) == lax.broadcasted_iota(
        jnp.int32, (cout, cout), 1
    )

    def column(ref):
        return jnp.sum(jnp.where(eye, ref[...], 0.0), axis=1, keepdims=True)

    bias, head_bias = column(cb), column(hb)
    depth = 9 * channels
    for k in range(3):
        w[k * cout : (k + 1) * cout, :] = cw[:, k * depth : (k + 1) * depth]

    def fetch(s, o, x):
        i = LINKS.index(o)
        v = links[s, i]
        c = jnp.maximum(v, 0) // slots
        u = jnp.maximum(v, 0) % slots
        at = i * 8 + c
        entry = jnp.where(v < 0, ZERO * slots, table[0, at] + u)
        shift = lax.rem(table[1, at] + table[2, at] * x + 512, 256)
        return entry, shift

    def part(s, o, x):
        entry, shift = fetch(s, o, x)
        lands = (15 if o[1] == 1 else 0) * 16 + (15 if o[2] == 1 else 0)
        half = lax.rem(lands - shift + 256, 256) // 128
        got = pool[entry, :, pl.ds(pl.multiple_of(half * 128, 128), 128)]
        return pltpu.roll(got, lax.rem(shift, 128), 1)

    def build(stack, s, p, dx, centre):
        x = p - 1
        rows = {dy: part(s, (dx, dy, 0), x) for dy in (-1, 1)}
        for dz in (-1, 0, 1):
            mid = centre
            if dz:
                edge = col == (0 if dz == -1 else 15)
                entry, shift = fetch(s, (dx, 0, dz), x)
                mid = jnp.where(edge, pltpu.roll(pool[entry], shift, 1), pltpu.roll(centre, -dz % 256, 1))
            for dy in (-1, 0, 1):
                t = ((dy + 1) * 3 + dz + 1) * channels
                if dy == 0:
                    stack[t : t + channels, :] = mid
                    continue
                moved = pltpu.roll(mid, -16 * dy % 256, 1)
                strip = rows[dy]
                lanes = slice(0, 128) if dy == -1 else slice(128, 256)
                if dz:
                    strip = jnp.where(
                        edge[:, lanes], part(s, (dx, dy, dz), x), pltpu.roll(strip, -dz % 128, 1)
                    )
                other = slice(128, 256) if dy == -1 else slice(0, 128)
                stack[t : t + channels, other] = moved[:, other]
                stack[t : t + channels, lanes] = jnp.where(
                    row[:, lanes] == (0 if dy == -1 else 15), strip, moved[:, lanes]
                )

    def multiply(stack, p):
        y = jnp.dot(w[...], stack[...], preferred_element_type=jnp.float32)
        for k in range(3):
            acc[p + 2 - k] += y[k * cout : (k + 1) * cout]

    def per_slot(s, _):
        acc[...] = jnp.zeros_like(acc)

        def shell(stack, p, dx):
            entry, _shift = fetch(s, (dx, 0, 0), 0)
            build(stack, s, p, dx, pool[entry])

        def inside(stack, p):
            at = pl.multiple_of((p - 1) * 256, 256)
            build(stack, s, p, 0, blk[s, :, pl.ds(at, 256)])

        shell(even, 0, -1)

        def inner(k, carry):
            inside(odd, 2 * k + 1)
            multiply(even, 2 * k)
            inside(even, 2 * k + 2)
            multiply(odd, 2 * k + 1)
            return carry

        lax.fori_loop(0, 8, inner, 0)
        shell(odd, 17, 1)
        multiply(even, 16)
        multiply(odd, 17)
        used = s < count[0]

        def finish(x, carry):
            hidden = jnp.maximum(acc[x + 2] + bias, 0.0).astype(jnp.bfloat16)
            mixed = jnp.dot(hw[...], hidden, preferred_element_type=jnp.float32) + head_bias
            mixed = jnp.where(used, mixed, 0.0)
            out[s, :, pl.ds(pl.multiple_of(x * 256, 256), 256)] = mixed.astype(out.dtype)
            return carry

        lax.fori_loop(0, 16, finish, 0, unroll=4)
        return 0

    lax.fori_loop(0, slots, per_slot, 0)


def body(sizes, blocks, block_count, neighbours, conv_weight, conv_bias, head_weight, head_bias):
    slots, channels, voxels = blocks.shape[2:]
    cout = head_weight.shape[0]
    blk = blocks.reshape(slots, channels, voxels)
    vmem = pl.BlockSpec(memory_space=pltpu.VMEM)
    smem = pl.BlockSpec(memory_space=pltpu.SMEM)
    pool = pl.pallas_call(
        functools.partial(exchange_kernel, sizes, slots),
        out_shape=jax.ShapeDtypeStruct((ZERO + 1, slots, channels, 256), blocks.dtype),
        in_specs=[vmem],
        out_specs=vmem,
        scratch_shapes=[
            pltpu.VMEM((12, channels, 128), blocks.dtype),
            pltpu.VMEM((27, channels, 128), blocks.dtype),
            pltpu.SemaphoreType.DMA((27,)),
            pltpu.SemaphoreType.DMA((27,)),
        ],
        compiler_params=pltpu.CompilerParams(collective_id=0, has_side_effects=True, vmem_limit_bytes=16 << 20),
        name="exchange",
    )(blk)
    out = pl.pallas_call(
        functools.partial(conv_kernel, slots),
        out_shape=jax.ShapeDtypeStruct((slots, cout, voxels), jnp.bfloat16),
        in_specs=[smem] * 3 + [vmem] * 6,
        out_specs=vmem,
        scratch_shapes=[
            pltpu.VMEM((3 * cout, 9 * channels), jnp.bfloat16),
            pltpu.VMEM((20, cout, 256), jnp.float32),
            pltpu.VMEM((9 * channels, 256), jnp.bfloat16),
            pltpu.VMEM((9 * channels, 256), jnp.bfloat16),
        ],
        compiler_params=pltpu.CompilerParams(vmem_limit_bytes=20 << 20),
        name="conv",
    )(
        block_count.reshape(1),
        neighbours.reshape(slots, 26),
        jnp.asarray(link_tables(slots)),
        blk,
        pool.reshape((ZERO + 1) * slots, channels, 256),
        conv_weight,
        conv_bias[None],
        head_weight,
        head_bias[None],
    )
    return out.reshape(1, 1, slots, cout, voxels)


def solution(mesh):
    placed = (
        P("gx", "gz", "gy", None, None),
        P("gx", "gz", "gy"),
        P("gx", "gz", "gy", None),
        P(),
        P(),
        P(),
        P(),
    )
    return jax.shard_map(
        functools.partial(body, dict(mesh.shape)),
        mesh=mesh,
        in_specs=placed,
        out_specs=P("gx", "gz", "gy", None, None),
        check_vma=False,
    )
```
